32 devices in a mesh: section: 4 (over z), expert: 4 (over y, x), dp: 2 (over core).
Axes of the slice: x: 2, y: 2, z: 4, core: 2. Of those that a mesh axis runs over, the one named last changes fastest.
Arguments:
- tokens: bfloat16 [2, 512, 2048], P(None, ('expert', 'dp')), may hold values from -24 to 24
- expert_ids: int32 [4, 2, 512, 4], P('section', None, ('expert', 'dp')), may hold values from 0 to 7, all different within a row; in each aligned block of 64 rows (0 to 63, 64 to 127, ..., all dimensions but the last counted through in order) at most 64 rows name the same one
- labels: int32 [2, 512], P(None, ('expert', 'dp')), may hold values from 0 to 127
- router: bfloat16 [4, 2048, 8], P('section'), may hold values from -0.125 to 0.125
- class_head: bfloat16 [2048, 128], replicated, may hold values from -0.5 to 0.5
- w_gate: bfloat16 [4, 8, 2048, 768], P('section', ('expert', 'dp')), may hold values from -0.125 to 0.125
- w_up: bfloat16 [4, 8, 2048, 768], P('section', ('expert', 'dp')), may hold values from -0.125 to 0.125
- w_down: bfloat16 [4, 8, 768, 2048], P('section', ('expert', 'dp')), may hold values from -0.21875 to 0.21875
Outputs:
- mean_loss: float32 [], replicated
- grad_head: float32 [2048, 128], replicated
- grad_router: float32 [4, 2048, 8], P('section')
- grad_gate: bfloat16 [4, 8, 2048, 768], P('section', ('expert', 'dp'))
- grad_up: bfloat16 [4, 8, 2048, 768], P('section', ('expert', 'dp'))
- grad_down: bfloat16 [4, 8, 768, 2048], P('section', ('expert', 'dp'))
The draws below stay inside these ranges and needn't reach their ends.
Inputs may be any that keep to these rules, and one draw needn't show every extreme that they name: `expert_ids`: each token names 4 different experts; among the 64 tokens of one device in one micro-batch and layer no expert is named more than 64 times, a bound that some block reaches.
All inputs are finite; a program needn't handle non-finite values.
Results may differ from the reference program's by a relative error of at most 0.025.
Values may be sent and summed in bfloat16 or wider, within the bound.
A program may use at most 320 MiB of HBM per device.

```python
import math
import jax
import jax.numpy as jnp
import numpy as np
from jax import lax

D = 2048
FFE = 768
NCLASS = 128
TOPK = 4
MB = 2
TOK_MB = 64
EXPERTS = 8
TOKENS = 512
CAP = 64
N_SECTION = 4


def draw_tokens(key, part):
    key_cols, key_rows, key_base = jax.random.split(key, 3)
    col_scale = jnp.exp(jax.random.uniform(key_cols, (1, 1, D), jnp.float32, math.log(0.3), math.log(3.0)))
    row_scale = jnp.exp(jax.random.uniform(key_rows, (MB, TOKENS, 1), jnp.float32, math.log(0.5), math.log(2.0)))
    base_draw = jax.random.normal(key_base, (MB, TOKENS, D), jnp.float32)
    return jnp.clip(base_draw * row_scale * col_scale, -24.0, 24.0).astype(jnp.bfloat16)


def with_ends(values, rng, smallest, high):
    extent = values.shape
    place = [jax.random.randint(jax.random.fold_in(rng, axis), (), 0, extent[axis]) for axis in range(len(extent))]
    values = values.at[tuple(place)].set(smallest)
    longest = extent.index(max(extent))
    place[longest] = (place[longest] + 1) % extent[longest]
    return values.at[tuple(place)].set(high)


def block_levels(stream_key, shape, pieces, least, largest):
    def one(position, blocks):
        draws = jax.random.uniform(jax.random.fold_in(jax.random.fold_in(stream_key, 6), position), (blocks,), jnp.float32, least / len(pieces), largest / len(pieces))
        return jnp.repeat(jnp.exp(draws), shape[position] // blocks).reshape((-1,) + (1,) * (len(shape) - position - 1))

    loudness = one(*pieces[0])
    for cut in pieces[1:]:
        loudness = loudness * one(*cut)
    return loudness


def deal_out(own_key, own, number, rows, count, top, most, slope):
    ranking = jax.random.permutation(own_key, count)
    crowded, common = portions_of(count, rows * top, most, slope, True), portions_of(count, rows * top, most, slope, False)
    places = jnp.arange(count)

    def named(lengths, rotation):
        used = int((lengths > 0).sum())
        fixed = max(1, used // 4)
        shifted = fixed + (places - fixed + rotation * (used - fixed)) % max(1, count - fixed)
        return jnp.zeros((count,), jnp.int32).at[ranking[jnp.where(places < fixed, places, shifted)]].set(jnp.asarray(lengths, jnp.int32))

    lengths = jnp.where(number % 4 == 0, named(crowded, number // 4), named(common, number - number // 4 - 1))
    mixed = jax.random.permutation(jax.random.fold_in(own, 3), count)
    source_of, taker = mixed[0:count // 2 * 2:2], mixed[1:count // 2 * 2:2]
    margin = jnp.minimum(lengths[source_of] - 1, most - lengths[taker]) // 2
    margin = jnp.where((source_of == ranking[0]) | (taker == ranking[0]) | (lengths[taker] == 0), 0, jnp.maximum(margin, 0))
    shifted = jax.random.randint(jax.random.fold_in(own, 4), (count // 2,), 0, 1 << 20) % (margin + 1)
    lengths = lengths.at[source_of].add(-shifted).at[taker].add(shifted)
    items = jnp.searchsorted(jnp.cumsum(lengths), jnp.arange(rows * top), side="right").astype(jnp.int32)
    table = items.reshape(top, rows).T
    table = table[jax.random.permutation(jax.random.fold_in(own, 1), rows)]
    rotation = jax.random.randint(jax.random.fold_in(own, 2), (rows, 1), 0, top)
    return jnp.take_along_axis(table, (jnp.arange(top)[None, :] + rotation) % top, axis=1)


def portions_of(number_of, total, bound, slope, full):
    weights = [(1 << 20) // math.isqrt(standing ** slope) + 1 for standing in range(1, number_of + 1)]
    largest = bound if full else min(bound, max(-(-total // number_of), total * weights[0] // sum(weights)))
    least = 1 if total - largest >= number_of - 1 else 0
    holding, spare = [largest] + [least] * (number_of - 1), total - largest - least * (number_of - 1)
    while spare > 0:
        candidates = [i for i in range(1, number_of) if holding[i] < largest] or [i for i in range(1, number_of) if holding[i] < bound]
        pool, remaining = sum([weights[i] for i in candidates]), spare
        for i in candidates:
            extra = min(bound - holding[i], max(1, remaining * weights[i] // pool), spare)
            holding[i] = holding[i] + extra
            spare = spare - extra
    return np.array(holding)


def scatter_about(own_key, shape, scale, most, pieces=(), kind=jnp.bfloat16):
    gain = block_levels(own_key, shape, pieces, -0.22, 0.18) if pieces else 1.0
    result = jax.random.normal(own_key, shape, jnp.float32) * scale * gain
    return jnp.minimum(jnp.maximum(result, -most), most).astype(kind)


def setup_inputs(seed: int = 0) -> dict:
    seeds = jax.random.split(jax.random.key(seed), 9)
    tokens = draw_tokens(jax.random.fold_in(seeds[8], 71), 0)
    expert_ids_keys = jax.random.split(jax.random.fold_in(seeds[1], 1), N_SECTION * MB * TOKENS // TOK_MB)
    expert_ids_turns = jax.random.permutation(jax.random.fold_in(seeds[1], 3), N_SECTION * MB * TOKENS // TOK_MB)
    expert_ids = jax.vmap(lambda own, number: deal_out(jax.random.fold_in(seeds[1], 2), own, number, TOK_MB, EXPERTS, TOPK, CAP, 2))(expert_ids_keys, expert_ids_turns).reshape((N_SECTION, MB, TOKENS, TOPK))
    labels = with_ends(jax.random.randint(seeds[2], (MB, TOKENS), 0, NCLASS), jax.random.fold_in(seeds[2], 1), 0, NCLASS - 1).astype(jnp.int32)
    router = scatter_about(seeds[3], (N_SECTION, D, EXPERTS), D ** -0.5, 0.125, ((0, 4),))
    class_head = scatter_about(seeds[4], (D, NCLASS), (D // 16) ** -0.5, 0.5)
    w_gate = scatter_about(seeds[5], (N_SECTION, EXPERTS, D, FFE), D ** -0.5, 0.125, ((0, 4), (1, 8)))
    w_up = scatter_about(seeds[6], (N_SECTION, EXPERTS, D, FFE), D ** -0.5, 0.125, ((0, 4), (1, 8)))
    w_down = scatter_about(seeds[7], (N_SECTION, EXPERTS, FFE, D), FFE ** -0.5, 0.21875, ((0, 4), (1, 8)))
    return dict(tokens=tokens, expert_ids=expert_ids, labels=labels, router=router, class_head=class_head, w_gate=w_gate, w_up=w_up, w_down=w_down)


soft_cap = 30.0
norm_eps = 1e-06

def capped(values):
    return soft_cap * jnp.tanh(values / soft_cap)

def normalize(layer_in):
    hidden_f = layer_in.astype(jnp.float32)
    inv_rms = lax.rsqrt(lax.optimization_barrier(jnp.mean(hidden_f * hidden_f, axis=-1, keepdims=True)) + norm_eps)
    return (hidden_f, inv_rms, (hidden_f * inv_rms).astype(jnp.bfloat16))

def gate_probs(normed, ids_now, router_w):
    logits = jnp.dot(normed, router_w, preferred_element_type=jnp.float32)
    one_hot = (ids_now[:, :, None] == jnp.arange(router_w.shape[1], dtype=jnp.int32)[None, None, :]).astype(jnp.float32)
    chosen = capped(lax.optimization_barrier(jnp.sum(one_hot * logits[:, None, :], axis=-1)))
    weights = jnp.exp(chosen)
    return (one_hot, chosen, weights / lax.optimization_barrier(jnp.sum(weights, axis=-1, keepdims=True)))

def expert_lists(flat_ids):

    def pick_rows(expert):
        return jnp.nonzero(flat_ids == expert, size=CAP * EXPERTS, fill_value=flat_ids.shape[0])[0].astype(jnp.int32)
    return lax.map(pick_rows, jnp.arange(EXPERTS, dtype=jnp.int32))

def contract_first(left, right):
    return lax.dot_general(left, right, (((0,), (0,)), ((), ())), preferred_element_type=jnp.float32)

def contract_last(left, right):
    return lax.dot_general(left, right, (((1,), (1,)), ((), ())), preferred_element_type=jnp.float32)

def moe_forward(layer_in, ids_now, router_w, gate_w, up_w, down_w):
    hidden_f, inv_rms, normed = normalize(layer_in)
    one_hot, chosen, probs = gate_probs(normed, ids_now, router_w)
    row_total = ids_now.shape[0] * TOPK
    row_lists = expert_lists(ids_now.reshape(-1))

    def one_expert(operands):
        picked, gate_e, up_e, down_e = operands
        tile_in = normed[jnp.minimum(picked, row_total - 1) // TOPK]
        gate_act = jnp.dot(tile_in, gate_e, preferred_element_type=jnp.float32)
        up_act = jnp.dot(tile_in, up_e, preferred_element_type=jnp.float32)
        hidden_act = (gate_act * jax.nn.sigmoid(gate_act) * up_act).astype(jnp.bfloat16)
        return jnp.dot(hidden_act, down_e, preferred_element_type=jnp.float32).astype(jnp.bfloat16)
    results = lax.map(one_expert, (row_lists, gate_w, up_w, down_w))
    expert_out = jnp.zeros((row_total, D), jnp.bfloat16).at[row_lists.reshape(-1)].set(results.reshape(-1, D), mode='drop')
    expert_out = expert_out.reshape(-1, TOPK, D)
    layer_out = (hidden_f + lax.optimization_barrier(jnp.sum(probs[:, :, None] * expert_out.astype(jnp.float32), axis=1))).astype(jnp.bfloat16)
    return (layer_out, expert_out)

def moe_backward(grad_out, layer_in, expert_out, ids_now, router_w, gate_w, up_w, down_w):
    hidden_f, inv_rms, normed = normalize(layer_in)
    one_hot, chosen, probs = gate_probs(normed, ids_now, router_w)
    grad_f = grad_out.astype(jnp.float32)
    grad_prob = lax.optimization_barrier(jnp.sum(grad_f[:, None, :] * expert_out.astype(jnp.float32), axis=-1))
    grad_rows = (probs[:, :, None] * grad_f[:, None, :]).astype(jnp.bfloat16).reshape(-1, D)
    row_total = grad_rows.shape[0]
    row_lists = expert_lists(ids_now.reshape(-1))

    def one_expert(operands):
        picked, gate_e, up_e, down_e = operands
        is_valid = (picked < row_total)[:, None]
        safe_rows = jnp.minimum(picked, row_total - 1)
        tile_in = jnp.where(is_valid, normed[safe_rows // TOPK], jnp.zeros((), jnp.bfloat16))
        tile_grad = jnp.where(is_valid, grad_rows[safe_rows], jnp.zeros((), jnp.bfloat16))
        gate_act = jnp.dot(tile_in, gate_e, preferred_element_type=jnp.float32)
        up_act = jnp.dot(tile_in, up_e, preferred_element_type=jnp.float32)
        sigmoid_gate = jax.nn.sigmoid(gate_act)
        silu_gate = gate_act * sigmoid_gate
        hidden_act = (silu_gate * up_act).astype(jnp.bfloat16)
        grad_down_e = contract_first(hidden_act, tile_grad)
        grad_hidden = contract_last(tile_grad, down_e)
        grad_gate_act = (grad_hidden * up_act * sigmoid_gate * (1.0 + gate_act * (1.0 - sigmoid_gate))).astype(jnp.bfloat16)
        grad_up_act = (grad_hidden * silu_gate).astype(jnp.bfloat16)
        grad_gate_e = contract_first(tile_in, grad_gate_act)
        grad_up_e = contract_first(tile_in, grad_up_act)
        grad_in_rows = (contract_last(grad_gate_act, gate_e) + contract_last(grad_up_act, up_e)).astype(jnp.bfloat16)
        return (grad_gate_e, grad_up_e, grad_down_e, grad_in_rows)
    grad_gate, grad_up, grad_down, grad_in_rows = lax.map(one_expert, (row_lists, gate_w, up_w, down_w))
    grad_parts = jnp.zeros((row_total, D), jnp.bfloat16).at[row_lists.reshape(-1)].set(grad_in_rows.reshape(-1, D), mode='drop')
    grad_parts = grad_parts.reshape(-1, TOPK, D)
    scaled = chosen / soft_cap
    grad_chosen = probs * (grad_prob - lax.optimization_barrier(jnp.sum(probs * grad_prob, axis=-1, keepdims=True))) * (1.0 - scaled * scaled)
    grad_route = lax.optimization_barrier(jnp.sum(grad_chosen[:, :, None] * one_hot, axis=1)).astype(jnp.bfloat16)
    grad_router = contract_first(normed, grad_route)
    grad_normed = lax.optimization_barrier(jnp.sum(grad_parts.astype(jnp.float32), axis=1)) + contract_last(grad_route, router_w)
    normed_f = hidden_f * inv_rms
    grad_in = (grad_f + inv_rms * (grad_normed - normed_f * lax.optimization_barrier(jnp.mean(grad_normed * normed_f, axis=-1, keepdims=True)))).astype(jnp.bfloat16)
    return (grad_in, grad_router, grad_gate, grad_up, grad_down)

def reference(tokens, expert_ids, labels, router, class_head, w_gate, w_up, w_down):
    section_inputs = []
    section_outputs = []
    finals = []
    for micro_num in range(MB):
        layer_in = tokens[micro_num]
        saved_in = []
        saved_out = []
        for section_num in range(N_SECTION):
            saved_in.append(layer_in)
            layer_in, expert_out = moe_forward(layer_in, expert_ids[section_num, micro_num], router[section_num], w_gate[section_num], w_up[section_num], w_down[section_num])
            saved_out.append(expert_out)
        section_inputs.append(saved_in)
        section_outputs.append(saved_out)
        finals.append(layer_in)
    final_rows = jnp.stack(finals).reshape(-1, D)
    class_logits = capped(jnp.dot(final_rows, class_head, preferred_element_type=jnp.float32))
    class_weights = jnp.exp(class_logits)
    class_total = lax.optimization_barrier(jnp.sum(class_weights, axis=-1, keepdims=True))
    label_hot = (labels.reshape(-1)[:, None] == jnp.arange(NCLASS, dtype=jnp.int32)[None, :]).astype(jnp.float32)
    mean_loss = jnp.mean(jnp.log(class_total[:, 0]) - lax.optimization_barrier(jnp.sum(label_hot * class_logits, axis=-1)))
    scaled = class_logits / soft_cap
    grad_logits = ((class_weights / class_total - label_hot) * (1.0 - scaled * scaled)).astype(jnp.bfloat16)
    grad_head = contract_first(final_rows, grad_logits)
    grad_top = contract_last(grad_logits, class_head).astype(jnp.bfloat16).reshape(MB, -1, D)
    grad_list = [grad_top[micro_num] for micro_num in range(MB)]
    router_list = []
    gate_list = []
    up_list = []
    down_list = []
    for section_num in reversed(range(N_SECTION)):
        router_sum = jnp.zeros((D, EXPERTS), jnp.float32)
        gate_sum = jnp.zeros((EXPERTS, D, FFE), jnp.float32)
        up_sum = jnp.zeros((EXPERTS, D, FFE), jnp.float32)
        down_sum = jnp.zeros((EXPERTS, FFE, D), jnp.float32)
        for micro_num in range(MB):
            grad_cur, grad_r, grad_g, grad_u, grad_d = moe_backward(grad_list[micro_num], section_inputs[micro_num][section_num], section_outputs[micro_num][section_num], expert_ids[section_num, micro_num], router[section_num], w_gate[section_num], w_up[section_num], w_down[section_num])
            grad_list[micro_num] = grad_cur
            router_sum = router_sum + grad_r
            gate_sum = gate_sum + grad_g
            up_sum = up_sum + grad_u
            down_sum = down_sum + grad_d
        router_list.append(router_sum)
        gate_list.append(gate_sum.astype(jnp.bfloat16))
        up_list.append(up_sum.astype(jnp.bfloat16))
        down_list.append(down_sum.astype(jnp.bfloat16))
    grad_router = jnp.stack(router_list[::-1])
    grad_gate = jnp.stack(gate_list[::-1])
    grad_up = jnp.stack(up_list[::-1])
    grad_down = jnp.stack(down_list[::-1])
    return (mean_loss, grad_head, grad_router, grad_gate, grad_up, grad_down)
```

```python
import functools

import jax
import jax.numpy as jnp
from jax import lax
from jax.experimental import pallas as pl
from jax.experimental.pallas import tpu as pltpu
from jax.sharding import PartitionSpec as P

soft_cap = 30.0
norm_eps = 1e-06
lanes = 128
MESH = pl.DeviceIdType.MESH
group = ("expert", "dp")


def capped(values):
    return soft_cap * jnp.tanh(values / soft_cap)


def dot_plain(left, right):
    return jnp.dot(left, right, preferred_element_type=jnp.float32)


def contract_first(left, right):
    return lax.dot_general(
        left, right, (((0,), (0,)), ((), ())), preferred_element_type=jnp.float32
    )


def contract_last(left, right):
    return lax.dot_general(
        left, right, (((1,), (1,)), ((), ())), preferred_element_type=jnp.float32
    )


def relay_kernel(sizes, chunks, step, first, carried_ref, root_ref, out_ref,
                 z_send, z_recv, own_sem, x_send, x_recv, d_send, d_recv, f_send, f_recv):
    sections, experts, cores = sizes
    s, e, d = lax.axis_index("section"), lax.axis_index("expert"), lax.axis_index("dp")
    last = sections - 1 - first
    me = e * cores + d
    rows = carried_ref.shape[0] // chunks

    barrier = pltpu.get_barrier_semaphore()
    for off in range(1, experts):
        pl.semaphore_signal(barrier, inc=1, device_id={"expert": lax.rem(e + off, experts)}, device_id_type=MESH)
    for off in range(1, cores):
        pl.semaphore_signal(barrier, inc=1, device_id={"dp": lax.rem(d + off, cores)}, device_id_type=MESH)

    @pl.when(s != first)
    def _():
        pl.semaphore_signal(barrier, inc=1, device_id={"section": s - step}, device_id_type=MESH)

    pl.semaphore_wait(barrier, experts + cores - 2 + (s != last).astype(jnp.int32))

    def part(c):
        return pl.ds(c * rows, rows)

    def shift(c):
        return pltpu.make_async_remote_copy(
            src_ref=carried_ref.at[part(c)], dst_ref=out_ref.at[me, part(c)],
            send_sem=z_send.at[c], recv_sem=z_recv.at[c],
            device_id={"section": lax.rem(s + step + sections, sections)}, device_id_type=MESH)

    def local(c):
        return pltpu.make_async_copy(root_ref.at[part(c)], out_ref.at[me, part(c)], own_sem.at[c])

    def across(c, off):
        return pltpu.make_async_remote_copy(
            src_ref=out_ref.at[me, part(c)], dst_ref=out_ref.at[me, part(c)],
            send_sem=x_send.at[c, off - 1], recv_sem=x_recv.at[c, off - 1],
            device_id={"expert": lax.rem(e + off, experts)}, device_id_type=MESH)

    def beside(c, off):
        return pltpu.make_async_remote_copy(
            src_ref=out_ref.at[me, part(c)], dst_ref=out_ref.at[me, part(c)],
            send_sem=d_send.at[c, off - 1], recv_sem=d_recv.at[c, off - 1],
            device_id={"dp": lax.rem(d + off, cores)}, device_id_type=MESH)

    def onward(c, off, far):
        source = lax.rem(e - far + experts, experts) * cores + d
        return pltpu.make_async_remote_copy(
            src_ref=out_ref.at[source, part(c)], dst_ref=out_ref.at[source, part(c)],
            send_sem=f_send.at[c, off - 1, far - 1], recv_sem=f_recv.at[c, off - 1, far - 1],
            device_id={"dp": lax.rem(d + off, cores)}, device_id_type=MESH)

    @pl.when(s != last)
    def _():
        for c in range(chunks):
            shift(c).start()

    @pl.when(s == first)
    def _():
        for c in range(chunks):
            local(c).start()

    for c in range(chunks):
        @pl.when(s == first)
        def _():
            local(c).wait()

        @pl.when(s != first)
        def _():
            shift(c).wait_recv()

        for off in range(1, experts):
            across(c, off).start()
        for off in range(1, cores):
            beside(c, off).start()
    for c in range(chunks):
        for far in range(1, experts):
            across(c, far).wait_recv()
            for off in range(1, cores):
                onward(c, off, far).start()
    for c in range(chunks):
        for off in range(1, cores):
            beside(c, off).wait()
            for far in range(1, experts):
                onward(c, off, far).wait()
        for off in range(1, experts):
            across(c, off).wait_send()

    @pl.when(s != last)
    def _():
        for c in range(chunks):
            shift(c).wait_send()


def relay(sizes, carried, root, step, first, call_id):
    sections, experts, cores = sizes
    rows, width = carried.shape
    chunks = 4 if rows % 64 == 0 else 1
    dma = pltpu.SemaphoreType.DMA
    out = pl.pallas_call(
        functools.partial(relay_kernel, sizes, chunks, step, first),
        out_shape=jax.ShapeDtypeStruct((experts * cores, rows, width), carried.dtype),
        in_specs=[pl.BlockSpec(memory_space=pltpu.VMEM)] * 2,
        out_specs=pl.BlockSpec(memory_space=pltpu.VMEM),
        scratch_shapes=[
            dma((chunks,)), dma((chunks,)), dma((chunks,)),
            dma((chunks, experts - 1)), dma((chunks, experts - 1)),
            dma((chunks, cores - 1)), dma((chunks, cores - 1)),
            dma((chunks, cores - 1, experts - 1)), dma((chunks, cores - 1, experts - 1)),
        ],
        compiler_params=pltpu.CompilerParams(collective_id=call_id, has_side_effects=True),
    )(carried, root)
    return out.reshape(experts * cores * rows, width)


def give_back_kernel(sizes, parts_ref, out_ref, own_sem, send_sem, recv_sem):
    sections, experts, cores = sizes
    e, d = lax.axis_index("expert"), lax.axis_index("dp")
    me = e * cores + d
    peers = [(x, c) for x in range(experts) for c in range(cores) if (x, c) != (0, 0)]

    def place(x, c):
        return lax.rem(e + x, experts), lax.rem(d + c, cores)

    barrier = pltpu.get_barrier_semaphore()
    for x, c in peers:
        to_e, to_d = place(x, c)
        pl.semaphore_signal(barrier, inc=1, device_id={"expert": to_e, "dp": to_d}, device_id_type=MESH)
    pl.semaphore_wait(barrier, len(peers))
    own = pltpu.make_async_copy(parts_ref.at[me], out_ref.at[me], own_sem)
    copies = []
    for n, (x, c) in enumerate(peers):
        to_e, to_d = place(x, c)
        copies.append(pltpu.make_async_remote_copy(
            src_ref=parts_ref.at[to_e * cores + to_d], dst_ref=out_ref.at[me],
            send_sem=send_sem.at[n], recv_sem=recv_sem.at[n],
            device_id={"expert": to_e, "dp": to_d}, device_id_type=MESH))
    for copy in copies:
        copy.start()
    own.start()
    own.wait()
    for copy in copies:
        copy.wait()


def give_back(sizes, parts, call_id):
    sections, experts, cores = sizes
    count = experts * cores
    dma = pltpu.SemaphoreType.DMA
    parts = parts.reshape(count, parts.shape[0] // count, parts.shape[1])
    return pl.pallas_call(
        functools.partial(give_back_kernel, sizes),
        out_shape=jax.ShapeDtypeStruct(parts.shape, parts.dtype),
        in_specs=[pl.BlockSpec(memory_space=pltpu.VMEM)],
        out_specs=pl.BlockSpec(memory_space=pltpu.VMEM),
        scratch_shapes=[dma(()), dma((count - 1,)), dma((count - 1,))],
        compiler_params=pltpu.CompilerParams(collective_id=call_id, has_side_effects=True),
    )(parts)


def shards(sizes, tokens, expert_ids, labels, router, class_head, w_gate, w_up, w_down):
    sections, experts, cores = sizes
    s = lax.axis_index("section")
    me = lax.axis_index("expert") * cores + lax.axis_index("dp")
    micro_count, tok_rows, width = tokens.shape
    router_w = router[0]
    router_t = router_w.T
    expert_count = router_w.shape[1]
    gate_w, up_w, down_w = w_gate[0, 0], w_up[0, 0], w_down[0, 0]
    hidden_dim = gate_w.shape[1]
    extra = (expert_count + lanes - 1) // lanes * lanes
    both_w = jnp.concatenate(
        [gate_w, up_w, jnp.pad(router_w, ((0, 0), (0, extra - expert_count)))], axis=1)
    is_last = s == sections - 1
    ticks = micro_count + sections - 1

    ids_all = lax.all_gather(expert_ids[0], group, axis=1, tiled=True)
    picks = jnp.transpose(ids_all, (0, 2, 1))
    named = jnp.arange(expert_count, dtype=jnp.int32)
    masks = jnp.any(picks[:, :, None, :] == named[None, None, :, None], axis=1).astype(jnp.float32)

    def own(rows_all):
        return lax.dynamic_slice_in_dim(rows_all, me * tok_rows, tok_rows, 0)

    kept = []
    finals = []
    layer_out = jnp.zeros((tok_rows, width), jnp.bfloat16)
    for t in range(ticks):
        hidden_all = relay(sizes, layer_out, tokens[min(t, micro_count - 1)], 1, 0, 0)
        mask = lax.dynamic_index_in_dim(masks, jnp.clip(t - s, 0, micro_count - 1), 0, keepdims=False)
        hidden_f = hidden_all.astype(jnp.float32)
        inv_rms = lax.rsqrt(jnp.mean(hidden_f * hidden_f, axis=-1, keepdims=True) + norm_eps)
        normed = (hidden_f * inv_rms).astype(jnp.bfloat16)
        chosen = capped(contract_last(router_t, normed))
        weights = jnp.exp(chosen) * mask
        probs = weights / jnp.sum(weights, axis=0, keepdims=True)
        scaled = chosen / soft_cap
        slope = probs * (1.0 - scaled * scaled)
        mine = lax.dynamic_index_in_dim(probs, me, 0, keepdims=False)[:, None]
        gate_up = dot_plain(normed, both_w[:, : 2 * hidden_dim])
        gate_act, up_act = gate_up[:, :hidden_dim], gate_up[:, hidden_dim:]
        sig = jax.nn.sigmoid(gate_act)
        silu = gate_act * sig
        hidden_w = (mine * silu * up_act).astype(jnp.bfloat16)
        d_gate = (mine * up_act * sig * (1.0 + gate_act * (1.0 - sig))).astype(jnp.bfloat16)
        d_up = (mine * silu).astype(jnp.bfloat16)
        partial = dot_plain(hidden_w, down_w).astype(jnp.bfloat16)
        mix = jnp.sum(give_back(sizes, partial, 1).astype(jnp.float32), axis=0)
        layer_in = own(hidden_all)
        layer_out = (layer_in.astype(jnp.float32) + mix).astype(jnp.bfloat16)
        kept.append((layer_in, mix, normed, chosen, slope, hidden_w, d_gate, d_up))
        if t >= sections - 1:
            finals.append(layer_out)

    final_rows = jnp.concatenate(finals, axis=0)
    class_logits = capped(dot_plain(final_rows, class_head))
    class_weights = jnp.exp(class_logits)
    class_total = jnp.sum(class_weights, axis=-1, keepdims=True)
    label_hot = (
        labels.reshape(-1)[:, None] == jnp.arange(class_head.shape[1], dtype=jnp.int32)[None, :]
    ).astype(jnp.float32)
    token_loss = jnp.log(class_total[:, 0]) - jnp.sum(label_hot * class_logits, axis=-1)
    scaled = class_logits / soft_cap
    grad_logits = ((class_weights / class_total - label_hot) * (1.0 - scaled * scaled)).astype(
        jnp.bfloat16
    )
    head_term = jnp.where(is_last, contract_first(final_rows, grad_logits), 0.0)
    loss_term = jnp.where(is_last, jnp.sum(token_loss), 0.0)
    grad_top = contract_last(grad_logits, class_head).astype(jnp.bfloat16)
    grad_top = grad_top.reshape(micro_count, tok_rows, width)
    head_total, loss_total = lax.psum((head_term, loss_term), ("section",) + group)

    grads = [None] * ticks
    grad_in = jnp.zeros((tok_rows, width), jnp.bfloat16)
    for u in range(ticks):
        t = ticks - 1 - u
        layer_in, mix, normed, chosen, slope, hidden_w, d_gate, d_up = kept[t]
        grad_all = relay(
            sizes, grad_in, grad_top[max(micro_count - 1 - u, 0)], -1, sections - 1, 2)
        down_grad = contract_last(grad_all, down_w)
        grad_acts = jnp.concatenate(
            [(down_grad * d_gate).astype(jnp.bfloat16), (down_grad * d_up).astype(jnp.bfloat16)],
            axis=1)
        my_scaled = lax.dynamic_index_in_dim(chosen, me, 0, keepdims=False) / soft_cap
        gain = jnp.sum(down_grad * hidden_w.astype(jnp.float32), axis=-1) * (1.0 - my_scaled * my_scaled)
        route = jnp.where(
            jnp.arange(extra, dtype=jnp.int32)[None, :] == me, gain[:, None], 0.0
        ).astype(jnp.bfloat16)
        grad_f = own(grad_all).astype(jnp.float32)
        shared = jnp.sum(grad_f * mix, axis=-1)
        my_slope = lax.dynamic_slice_in_dim(slope, me * tok_rows, tok_rows, 1)
        common = (my_slope * shared[None, :]).astype(jnp.bfloat16)
        grads[t] = (normed, hidden_w, grad_all, grad_acts, route, common, own(normed))
        if u + 1 < ticks:
            partial = dot_plain(
                jnp.concatenate([grad_acts, route], axis=1), both_w.T
            ).astype(jnp.bfloat16)
            grad_normed = jnp.sum(give_back(sizes, partial, 1).astype(jnp.float32), axis=0)
            grad_normed = grad_normed - contract_first(common, router_t)
            hidden_f = layer_in.astype(jnp.float32)
            inv_rms = lax.rsqrt(jnp.mean(hidden_f * hidden_f, axis=-1, keepdims=True) + norm_eps)
            normed_f = hidden_f * inv_rms
            grad_in = (
                grad_f
                + inv_rms
                * (grad_normed - normed_f * jnp.mean(grad_normed * normed_f, axis=-1, keepdims=True))
            ).astype(jnp.bfloat16)

    def totals(begin):
        chosen_ticks = grads[begin : begin + micro_count]
        normed, hidden_w, grad_all, grad_acts, route, common, normed_own = [
            jnp.concatenate(parts, axis=1 if n == 5 else 0)
            for n, parts in enumerate(zip(*chosen_ticks))
        ]
        first = contract_first(route, normed)[:expert_count]
        return (
            first - dot_plain(common, normed_own),
            contract_first(normed, grad_acts[:, :hidden_dim]).astype(jnp.bfloat16),
            contract_first(normed, grad_acts[:, hidden_dim:]).astype(jnp.bfloat16),
            contract_first(hidden_w, grad_all).astype(jnp.bfloat16),
        )

    router_sum, grad_gate, grad_up, grad_down = lax.switch(
        s, [functools.partial(totals, begin) for begin in range(sections)])
    router_out = lax.psum(router_sum, group).T[None]
    mean_loss = loss_total / (micro_count * tok_rows * experts * cores)
    return (
        mean_loss,
        head_total,
        router_out,
        grad_gate[None, None],
        grad_up[None, None],
        grad_down[None, None],
    )


def solution(mesh):
    sizes = tuple(mesh.shape[axis] for axis in ("section", "expert", "dp"))
    return jax.shard_map(
        functools.partial(shards, sizes),
        mesh=mesh,
        in_specs=(
            P(None, ("expert", "dp"), None),
            P("section", None, ("expert", "dp"), None),
            P(None, ("expert", "dp")),
            P("section", None, None),
            P(),
            P("section", ("expert", "dp"), None, None),
            P("section", ("expert", "dp"), None, None),
            P("section", ("expert", "dp"), None, None),
        ),
        out_specs=(
            P(),
            P(),
            P("section", None, None),
            P("section", ("expert", "dp"), None, None),
            P("section", ("expert", "dp"), None, None),
            P("section", ("expert", "dp"), None, None),
        ),
        check_vma=False,
    )
```

```python
import functools

import jax
import jax.numpy as jnp
from jax import lax
from jax.experimental import pallas as pl
from jax.experimental.pallas import tpu as pltpu
from jax.sharding import PartitionSpec as P

soft_cap = 30.0
norm_eps = 1e-06
lanes = 128
MESH = pl.DeviceIdType.MESH
group = ("expert", "dp")


def capped(values):
    return soft_cap * jnp.tanh(values / soft_cap)


def dot_plain(left, right):
    return jnp.dot(left, right, preferred_element_type=jnp.float32)


def contract_first(left, right):
    return lax.dot_general(
        left, right, (((0,), (0,)), ((), ())), preferred_element_type=jnp.float32
    )


def contract_last(left, right):
    return lax.dot_general(
        left, right, (((1,), (1,)), ((), ())), preferred_element_type=jnp.float32
    )


def relay_kernel(sizes, chunks, step, first, carried_ref, root_ref, out_ref,
                 z_send, z_recv, own_sem, x_send, x_recv, d_send, d_recv, f_send, f_recv):
    sections, experts, cores = sizes
    s, e, d = lax.axis_index("section"), lax.axis_index("expert"), lax.axis_index("dp")
    last = sections - 1 - first
    me = e * cores + d
    rows = carried_ref.shape[0] // chunks

    barrier = pltpu.get_barrier_semaphore()
    for off in range(1, experts):
        pl.semaphore_signal(barrier, inc=1, device_id={"expert": lax.rem(e + off, experts)}, device_id_type=MESH)
    for off in range(1, cores):
        pl.semaphore_signal(barrier, inc=1, device_id={"dp": lax.rem(d + off, cores)}, device_id_type=MESH)

    @pl.when(s != first)
    def _():
        pl.semaphore_signal(barrier, inc=1, device_id={"section": s - step}, device_id_type=MESH)

    pl.semaphore_wait(barrier, experts + cores - 2 + (s != last).astype(jnp.int32))

    def part(c):
        return pl.ds(c * rows, rows)

    def shift(c):
        return pltpu.make_async_remote_copy(
            src_ref=carried_ref.at[part(c)], dst_ref=out_ref.at[me, part(c)],
            send_sem=z_send.at[c], recv_sem=z_recv.at[c],
            device_id={"section": lax.rem(s + step + sections, sections)}, device_id_type=MESH)

    def local(c):
        return pltpu.make_async_copy(root_ref.at[part(c)], out_ref.at[me, part(c)], own_sem.at[c])

    def across(c, off):
        return pltpu.make_async_remote_copy(
            src_ref=out_ref.at[me, part(c)], dst_ref=out_ref.at[me, part(c)],
            send_sem=x_send.at[c, off - 1], recv_sem=x_recv.at[c, off - 1],
            device_id={"expert": lax.rem(e + off, experts)}, device_id_type=MESH)

    def beside(c, off):
        return pltpu.make_async_remote_copy(
            src_ref=out_ref.at[me, part(c)], dst_ref=out_ref.at[me, part(c)],
            send_sem=d_send.at[c, off - 1], recv_sem=d_recv.at[c, off - 1],
            device_id={"dp": lax.rem(d + off, cores)}, device_id_type=MESH)

    def onward(c, off, far):
        source = lax.rem(e - far + experts, experts) * cores + d
        return pltpu.make_async_remote_copy(
            src_ref=out_ref.at[source, part(c)], dst_ref=out_ref.at[source, part(c)],
            send_sem=f_send.at[c, off - 1, far - 1], recv_sem=f_recv.at[c, off - 1, far - 1],
            device_id={"dp": lax.rem(d + off, cores)}, device_id_type=MESH)

    @pl.when(s != last)
    def _():
        for c in range(chunks):
            shift(c).start()

    @pl.when(s == first)
    def _():
        for c in range(chunks):
            local(c).start()

    for c in range(chunks):
        @pl.when(s == first)
        def _():
            local(c).wait()

        @pl.when(s != first)
        def _():
            shift(c).wait_recv()

        for off in range(1, experts):
            across(c, off).start()
        for off in range(1, cores):
            beside(c, off).start()
    for c in range(chunks):
        for far in range(1, experts):
            across(c, far).wait_recv()
            for off in range(1, cores):
                onward(c, off, far).start()
    for c in range(chunks):
        for off in range(1, cores):
            beside(c, off).wait()
            for far in range(1, experts):
                onward(c, off, far).wait()
        for off in range(1, experts):
            across(c, off).wait_send()

    @pl.when(s != last)
    def _():
        for c in range(chunks):
            shift(c).wait_send()


def relay(sizes, carried, root, step, first, call_id):
    sections, experts, cores = sizes
    rows, width = carried.shape
    chunks = 4 if rows % 64 == 0 else 1
    dma = pltpu.SemaphoreType.DMA
    out = pl.pallas_call(
        functools.partial(relay_kernel, sizes, chunks, step, first),
        out_shape=jax.ShapeDtypeStruct((experts * cores, rows, width), carried.dtype),
        in_specs=[pl.BlockSpec(memory_space=pltpu.VMEM)] * 2,
        out_specs=pl.BlockSpec(memory_space=pltpu.VMEM),
        scratch_shapes=[
            dma((chunks,)), dma((chunks,)), dma((chunks,)),
            dma((chunks, experts - 1)), dma((chunks, experts - 1)),
            dma((chunks, cores - 1)), dma((chunks, cores - 1)),
            dma((chunks, cores - 1, experts - 1)), dma((chunks, cores - 1, experts - 1)),
        ],
        cost_estimate=pl.CostEstimate(
            flops=0, bytes_accessed=30 * experts * cores * carried.size * 2, transcendentals=0),
        compiler_params=pltpu.CompilerParams(collective_id=call_id, has_side_effects=True),
    )(carried, root)
    return out.reshape(experts * cores * rows, width)


def give_back_kernel(sizes, parts_ref, out_ref, stage_ref, sum_ref, d_send, d_recv, x_send, x_recv):
    sections, experts, cores = sizes
    e, d = lax.axis_index("expert"), lax.axis_index("dp")

    barrier = pltpu.get_barrier_semaphore()
    for off in range(1, experts):
        pl.semaphore_signal(barrier, inc=1, device_id={"expert": lax.rem(e + off, experts)}, device_id_type=MESH)
    for off in range(1, cores):
        pl.semaphore_signal(barrier, inc=1, device_id={"dp": lax.rem(d + off, cores)}, device_id_type=MESH)
    pl.semaphore_wait(barrier, experts + cores - 2)

    def beside(off, core_off):
        to_d = lax.rem(d + core_off, cores)
        return pltpu.make_async_remote_copy(
            src_ref=parts_ref.at[lax.rem(e + off, experts) * cores + to_d],
            dst_ref=stage_ref.at[core_off - 1, off],
            send_sem=d_send.at[core_off - 1, off], recv_sem=d_recv.at[core_off - 1, off],
            device_id={"dp": to_d}, device_id_type=MESH)

    def across(off):
        return pltpu.make_async_remote_copy(
            src_ref=sum_ref.at[off - 1], dst_ref=out_ref.at[e],
            send_sem=x_send.at[off - 1], recv_sem=x_recv.at[off - 1],
            device_id={"expert": lax.rem(e + off, experts)}, device_id_type=MESH)

    order = [off for off in range(experts - 1, 0, -1)] + [0]
    for off in order:
        for core_off in range(1, cores):
            beside(off, core_off).start()
    for n, off in enumerate(order):
        total = parts_ref[lax.rem(e + off, experts) * cores + d].astype(jnp.float32)
        for core_off in range(1, cores):
            beside(off, core_off).wait_recv()
            total = total + stage_ref[core_off - 1, off].astype(jnp.float32)
        if off == 0:
            out_ref[e] = total.astype(out_ref.dtype)
        else:
            sum_ref[off - 1] = total.astype(out_ref.dtype)
        if n > 0:
            across(order[n - 1]).start()
    for off in range(1, experts):
        across(off).wait()
    for off in order:
        for core_off in range(1, cores):
            beside(off, core_off).wait_send()


def give_back(sizes, parts, call_id):
    sections, experts, cores = sizes
    block = parts.shape[1:]
    dma = pltpu.SemaphoreType.DMA
    return pl.pallas_call(
        functools.partial(give_back_kernel, sizes),
        out_shape=jax.ShapeDtypeStruct((experts,) + block, parts.dtype),
        in_specs=[pl.BlockSpec(memory_space=pltpu.VMEM)],
        out_specs=pl.BlockSpec(memory_space=pltpu.VMEM),
        scratch_shapes=[
            pltpu.VMEM((cores - 1, experts) + block, parts.dtype),
            pltpu.VMEM((experts - 1,) + block, parts.dtype),
            dma((cores - 1, experts)), dma((cores - 1, experts)),
            dma((experts - 1,)), dma((experts - 1,)),
        ],
        cost_estimate=pl.CostEstimate(flops=0, bytes_accessed=30 * parts.size * 2, transcendentals=0),
        compiler_params=pltpu.CompilerParams(collective_id=call_id, has_side_effects=True),
    )(parts)


def shards(sizes, tokens, expert_ids, labels, router, class_head, w_gate, w_up, w_down):
    sections, experts, cores = sizes
    s = lax.axis_index("section")
    me = lax.axis_index("expert") * cores + lax.axis_index("dp")
    micro_count, tok_rows, width = tokens.shape
    router_w = router[0]
    router_t = router_w.T
    expert_count = router_w.shape[1]
    gate_w, up_w, down_w = w_gate[0, 0], w_up[0, 0], w_down[0, 0]
    hidden_dim = gate_w.shape[1]
    extra = (expert_count + lanes - 1) // lanes * lanes
    both_w = jnp.concatenate(
        [gate_w, up_w, jnp.pad(router_w, ((0, 0), (0, extra - expert_count)))], axis=1)
    is_last = s == sections - 1
    ticks = micro_count + sections - 1

    ids_all = lax.all_gather(expert_ids[0], group, axis=1, tiled=True)
    picks = jnp.transpose(ids_all, (0, 2, 1))
    named = jnp.arange(expert_count, dtype=jnp.int32)
    masks = jnp.any(picks[:, :, None, :] == named[None, None, :, None], axis=1).astype(jnp.float32)

    def own(rows_all):
        return lax.dynamic_slice_in_dim(rows_all, me * tok_rows, tok_rows, 0)

    def by_device(rows_all):
        return rows_all.reshape(experts * cores, tok_rows, width)

    kept = []
    finals = []
    layer_out = jnp.zeros((tok_rows, width), jnp.bfloat16)
    for t in range(ticks):
        hidden_all = relay(sizes, layer_out, tokens[min(t, micro_count - 1)], 1, 0, 0)
        mask = lax.dynamic_index_in_dim(masks, jnp.clip(t - s, 0, micro_count - 1), 0, keepdims=False)
        hidden_f = hidden_all.astype(jnp.float32)
        inv_rms = lax.rsqrt(jnp.mean(hidden_f * hidden_f, axis=-1, keepdims=True) + norm_eps)
        normed = (hidden_f * inv_rms).astype(jnp.bfloat16)
        chosen = capped(contract_last(router_t, normed))
        weights = jnp.exp(chosen) * mask
        probs = weights / jnp.sum(weights, axis=0, keepdims=True)
        scaled = chosen / soft_cap
        slope = probs * (1.0 - scaled * scaled)
        mine = lax.dynamic_index_in_dim(probs, me, 0, keepdims=False)[:, None]
        gate_up = dot_plain(normed, both_w[:, : 2 * hidden_dim])
        gate_act, up_act = gate_up[:, :hidden_dim], gate_up[:, hidden_dim:]
        sig = jax.nn.sigmoid(gate_act)
        silu = gate_act * sig
        hidden_w = (mine * silu * up_act).astype(jnp.bfloat16)
        d_gate = (mine * up_act * sig * (1.0 + gate_act * (1.0 - sig))).astype(jnp.bfloat16)
        d_up = (mine * silu).astype(jnp.bfloat16)
        partial = dot_plain(hidden_w, down_w).astype(jnp.bfloat16)
        mix = jnp.sum(give_back(sizes, by_device(partial), 1).astype(jnp.float32), axis=0)
        layer_in = own(hidden_all)
        layer_out = (layer_in.astype(jnp.float32) + mix).astype(jnp.bfloat16)
        kept.append((layer_in, mix, normed, chosen, slope, hidden_w, d_gate, d_up))
        if t >= sections - 1:
            finals.append(layer_out)

    final_rows = jnp.concatenate(finals, axis=0)
    class_logits = capped(dot_plain(final_rows, class_head))
    class_weights = jnp.exp(class_logits)
    class_total = jnp.sum(class_weights, axis=-1, keepdims=True)
    label_hot = (
        labels.reshape(-1)[:, None] == jnp.arange(class_head.shape[1], dtype=jnp.int32)[None, :]
    ).astype(jnp.float32)
    token_loss = jnp.log(class_total[:, 0]) - jnp.sum(label_hot * class_logits, axis=-1)
    scaled = class_logits / soft_cap
    grad_logits = ((class_weights / class_total - label_hot) * (1.0 - scaled * scaled)).astype(
        jnp.bfloat16
    )
    head_term = jnp.where(is_last, contract_first(final_rows, grad_logits), 0.0)
    loss_term = jnp.where(is_last, jnp.sum(token_loss), 0.0)
    grad_top = contract_last(grad_logits, class_head).astype(jnp.bfloat16)
    grad_top = grad_top.reshape(micro_count, tok_rows, width)
    loss_row = jnp.full((8, head_term.shape[1]), loss_term, jnp.float32)
    summed = lax.psum(jnp.concatenate([head_term, loss_row], axis=0), ("section",) + group)
    head_total, loss_total = summed[:width], summed[width, 0]

    grads = [None] * ticks
    grad_in = jnp.zeros((tok_rows, width), jnp.bfloat16)
    for u in range(ticks):
        t = ticks - 1 - u
        layer_in, mix, normed, chosen, slope, hidden_w, d_gate, d_up = kept[t]
        grad_all = relay(
            sizes, grad_in, grad_top[max(micro_count - 1 - u, 0)], -1, sections - 1, 2)
        down_grad = contract_last(grad_all, down_w)
        grad_acts = jnp.concatenate(
            [(down_grad * d_gate).astype(jnp.bfloat16), (down_grad * d_up).astype(jnp.bfloat16)],
            axis=1)
        my_scaled = lax.dynamic_index_in_dim(chosen, me, 0, keepdims=False) / soft_cap
        gain = jnp.sum(down_grad * hidden_w.astype(jnp.float32), axis=-1) * (1.0 - my_scaled * my_scaled)
        route = jnp.where(
            jnp.arange(extra, dtype=jnp.int32)[None, :] == me, gain[:, None], 0.0
        ).astype(jnp.bfloat16)
        grad_f = own(grad_all).astype(jnp.float32)
        shared = jnp.sum(grad_f * mix, axis=-1)
        my_slope = lax.dynamic_slice_in_dim(slope, me * tok_rows, tok_rows, 1)
        common = (my_slope * shared[None, :]).astype(jnp.bfloat16)
        grads[t] = (normed, hidden_w, grad_all, grad_acts, route, common, own(normed))
        if u + 1 < ticks:
            partial = dot_plain(
                jnp.concatenate([grad_acts, route], axis=1), both_w.T
            ).astype(jnp.bfloat16)
            grad_normed = jnp.sum(give_back(sizes, by_device(partial), 1).astype(jnp.float32), axis=0)
            grad_normed = grad_normed - contract_first(common, router_t)
            hidden_f = layer_in.astype(jnp.float32)
            inv_rms = lax.rsqrt(jnp.mean(hidden_f * hidden_f, axis=-1, keepdims=True) + norm_eps)
            normed_f = hidden_f * inv_rms
            grad_in = (
                grad_f
                + inv_rms
                * (grad_normed - normed_f * jnp.mean(grad_normed * normed_f, axis=-1, keepdims=True))
            ).astype(jnp.bfloat16)

    def totals(begin):
        chosen_ticks = grads[begin : begin + micro_count]
        normed, hidden_w, grad_all, grad_acts, route, common, normed_own = [
            jnp.concatenate(parts, axis=1 if n == 5 else 0)
            for n, parts in enumerate(zip(*chosen_ticks))
        ]
        first = contract_first(route, normed)[:expert_count]
        return (
            first - dot_plain(common, normed_own),
            contract_first(normed, grad_acts[:, :hidden_dim]).astype(jnp.bfloat16),
            contract_first(normed, grad_acts[:, hidden_dim:]).astype(jnp.bfloat16),
            contract_first(hidden_w, grad_all).astype(jnp.bfloat16),
        )

    router_sum, grad_gate, grad_up, grad_down = lax.switch(
        s, [functools.partial(totals, begin) for begin in range(sections)])
    copies = jnp.broadcast_to(router_sum[None], (experts * cores,) + router_sum.shape)
    router_out = jnp.sum(give_back(sizes, copies, 3), axis=0).T[None]
    mean_loss = loss_total / (micro_count * tok_rows * experts * cores)
    return (
        mean_loss,
        head_total,
        router_out,
        grad_gate[None, None],
        grad_up[None, None],
        grad_down[None, None],
    )


def solution(mesh):
    sizes = tuple(mesh.shape[axis] for axis in ("section", "expert", "dp"))
    return jax.shard_map(
        functools.partial(shards, sizes),
        mesh=mesh,
        in_specs=(
            P(None, ("expert", "dp"), None),
            P("section", None, ("expert", "dp"), None),
            P(None, ("expert", "dp")),
            P("section", None, None),
            P(),
            P("section", ("expert", "dp"), None, None),
            P("section", ("expert", "dp"), None, None),
            P("section", ("expert", "dp"), None, None),
        ),
        out_specs=(
            P(),
            P(),
            P("section", None, None),
            P("section", ("expert", "dp"), None, None),
            P("section", ("expert", "dp"), None, None),
            P("section", ("expert", "dp"), None, None),
        ),
        check_vma=False,
    )
```
